32 devices in a mesh: shard: 4 (over y, x), replica: 8 (over z, core).
Axes of the slice: x: 2, y: 2, z: 4, core: 2. Of those that a mesh axis runs over, the one named last changes fastest.
Arguments:
- tokens: bfloat16 [8192, 768], P(('shard', 'replica')), may hold values from -6 to 6
- cond: bfloat16 [32, 768], P(('shard', 'replica')), may hold values from -6 to 6
- cot: bfloat16 [8192, 768], P(('shard', 'replica')), may hold values from -6 to 6
- w_mod: bfloat16 [768, 4608], P('shard'), may hold values from -0.21875 to 0.21875
- b_mod: bfloat16 [4608], P('shard'), may hold values from -2.5 to 2.5
- w_qkv: bfloat16 [768, 2304], P('shard'), may hold values from -0.21875 to 0.21875
- b_qv: bfloat16 [1536], P('shard'), may hold values from -2.5 to 2.5
- w_out: bfloat16 [768, 768], P('shard'), may hold values from -0.875 to 0.875
- b_out: bfloat16 [768], P('shard'), may hold values from -2.5 to 2.5
- w_fc1: bfloat16 [768, 3072], P('shard'), may hold values from -0.21875 to 0.21875
- b_fc1: bfloat16 [3072], P('shard'), may hold values from -2.5 to 2.5
- w_fc2: bfloat16 [3072, 768], P('shard'), may hold values from -0.109375 to 0.109375
- b_fc2: bfloat16 [768], P('shard'), may hold values from -2.5 to 2.5
Outputs:
- mixed: bfloat16 [8192, 768], P(('shard', 'replica'))
- grad_tokens: float32 [8192, 768], P(('shard', 'replica'))
- grad_cond: float32 [32, 768], P(('shard', 'replica'))
- grad_w_mod: float32 [768, 4608], P('shard')
- grad_b_mod: float32 [4608], P('shard')
- grad_w_qkv: float32 [768, 2304], P('shard')
- grad_b_qv: float32 [1536], P('shard')
- grad_w_out: float32 [768, 768], P('shard')
- grad_b_out: float32 [768], P('shard')
- grad_w_fc1: float32 [768, 3072], P('shard')
- grad_b_fc1: float32 [3072], P('shard')
- grad_w_fc2: float32 [3072, 768], P('shard')
- grad_b_fc2: float32 [768], P('shard')
The draws below stay inside these ranges and needn't reach their ends.
All inputs are finite; a program needn't handle non-finite values.
Results may differ from the reference program's by a relative error of at most 0.015.
The reference program's roundings to bfloat16 on the way count: a program that leaves them out, or rounds other values in their place, can miss the bound.
Values may be sent and summed in bfloat16 or wider, within the bound.
No kernel may reach another device: no remote copies, remote signals or barrier semaphores. Data moves between devices by JAX's collectives and lax.ppermute only.
A program may use at most 192 MiB of HBM per device.

```python
import math
import jax
import jax.numpy as jnp
from jax import lax

D = 768
FF = 3072
LAT_TOK = 256
LATENTS = 32
TOKENS = 8192


def block_levels(key, dims, cuts, low, top_value):
    def one(axis_at, blocks):
        draws = jax.random.uniform(jax.random.fold_in(jax.random.fold_in(key, 6), axis_at), (blocks,), jnp.float32, low / len(cuts), top_value / len(cuts))
        return jnp.repeat(jnp.exp(draws), dims[axis_at] // blocks).reshape((-1,) + (1,) * (len(dims) - axis_at - 1))

    loudness = one(*cuts[0])
    for cut in cuts[1:]:
        loudness = loudness * one(*cut)
    return loudness


def gaussian(stream_key, dims, deviation, bound, cuts=(), dtype=jnp.bfloat16):
    drawn = jax.random.normal(stream_key, dims, jnp.float32) * deviation
    if len(cuts) > 0:
        drawn = block_levels(stream_key, dims, cuts, -0.22, 0.18) * drawn
    return jnp.clip(drawn, min=-bound, max=bound).astype(dtype)


def setup_inputs(seed: int = 0) -> dict:
    splits = jax.random.split(jax.random.key(seed), 14)
    tokens = gaussian(splits[0], (TOKENS, D), 1.0, 6.0, ((0, 32),))
    cond = gaussian(splits[1], (LATENTS, D), 1.0, 6.0, ((0, 32),))
    cot = gaussian(splits[2], (TOKENS, D), 1.0, 6.0, ((0, 32),))
    w_mod = gaussian(splits[3], (D, 6 * D), D ** -0.5, 0.21875, ((0, 4),))
    b_mod = gaussian(splits[4], (6 * D,), 0.4, 2.5, ((0, 4),))
    w_qkv = gaussian(splits[5], (D, 3 * D), D ** -0.5, 0.21875, ((0, 4),))
    b_qv = gaussian(splits[6], (2 * D,), 0.4, 2.5, ((0, 4),))
    w_out = gaussian(splits[7], (D, D), (D // 16) ** -0.5, 0.875, ((0, 4),))
    b_out = gaussian(splits[8], (D,), 0.4, 2.5, ((0, 4),))
    w_fc1 = gaussian(splits[9], (D, FF), D ** -0.5, 0.21875, ((0, 4),))
    b_fc1 = gaussian(splits[10], (FF,), 0.4, 2.5, ((0, 4),))
    w_fc2 = gaussian(splits[11], (FF, D), FF ** -0.5, 0.109375, ((0, 4),))
    b_fc2 = gaussian(splits[12], (D,), 0.4, 2.5, ((0, 4),))
    return dict(tokens=tokens, cond=cond, cot=cot, w_mod=w_mod, b_mod=b_mod, w_qkv=w_qkv, b_qv=b_qv, w_out=w_out, b_out=b_out, w_fc1=w_fc1, b_fc1=b_fc1, w_fc2=w_fc2, b_fc2=b_fc2)


def matmul(left, right):
    return jnp.dot(left, right, preferred_element_type=jnp.float32)

def matmul_tn(left, right):
    return lax.dot_general(left, right, (((0,), (0,)), ((), ())), preferred_element_type=jnp.float32)

def matmul_nt(left, right):
    return lax.dot_general(left, right, (((1,), (1,)), ((), ())), preferred_element_type=jnp.float32)

def batched(form, left, right):
    return jnp.einsum(form, left.astype(jnp.float32), right.astype(jnp.float32), precision=lax.Precision.HIGHEST)

def layer_norm(values):
    center = values - lax.optimization_barrier(jnp.mean(values, -1, keepdims=True))
    rstd_val = lax.rsqrt(lax.optimization_barrier(jnp.mean(center * center, -1, keepdims=True)) + 1e-06)
    return (center * rstd_val, rstd_val)

def norm_back(grad_norm, normed, rstd_val):
    return rstd_val * (grad_norm - lax.optimization_barrier(jnp.mean(grad_norm, -1, keepdims=True)) - normed * lax.optimization_barrier(jnp.mean(grad_norm * normed, -1, keepdims=True)))

def gelu_tanh(pre_value):
    return jax.nn.gelu(pre_value, approximate=True)

def block_pass(tokens, cond, cot, weights, fetch_back):
    w_mod, b_mod, w_qkv, b_qv, w_out, b_out, w_fc1, b_fc1, w_fc2, b_fc2 = weights
    latent_count, token_count, model_width = tokens.shape
    head_count = model_width // 64
    row_count = latent_count * token_count
    cond_f = cond.astype(jnp.float32)
    cond_act = jax.nn.silu(cond_f).astype(jnp.bfloat16)
    modulation = matmul(cond_act, w_mod) + b_mod.astype(jnp.float32)
    pieces = [modulation[:, offset * model_width:(offset + 1) * model_width][:, None, :] for offset in range(6)]
    shift_a, scale_a, gate_a, shift_b, scale_b, gate_b = pieces
    inputs = tokens.astype(jnp.float32)
    norm_a, rstd_a = layer_norm(inputs)
    modul_a = (norm_a * (1.0 + scale_a) + shift_a).astype(jnp.bfloat16).reshape(row_count, model_width)
    projected = matmul(modul_a, w_qkv)
    bias_qv = b_qv.astype(jnp.float32)
    head_shape = (latent_count, token_count, head_count, 64)
    queries = (projected[:, :model_width] + bias_qv[:model_width]).astype(jnp.bfloat16).reshape(head_shape)
    keys_b = projected[:, model_width:2 * model_width].astype(jnp.bfloat16).reshape(head_shape)
    values_b = (projected[:, 2 * model_width:] + bias_qv[model_width:]).astype(jnp.bfloat16).reshape(head_shape)
    scores = batched('lqhd,lkhd->lhqk', queries, keys_b) * 0.125
    row_max = lax.optimization_barrier(jnp.max(scores, -1, keepdims=True))
    exp_scores = jnp.exp(scores - row_max)
    row_total = lax.optimization_barrier(jnp.sum(exp_scores, -1, keepdims=True))
    log_total = row_max + jnp.log(row_total)
    attn_probs = (exp_scores / row_total).astype(jnp.bfloat16)
    attended = batched('lhqk,lkhd->lqhd', attn_probs, values_b).astype(jnp.bfloat16)
    attn_flat = attended.reshape(row_count, model_width)
    branch_a = (matmul(attn_flat, w_out) + b_out.astype(jnp.float32)).reshape(latent_count, token_count, model_width)
    middle = inputs + gate_a * branch_a
    norm_b, rstd_b = layer_norm(middle)
    modul_b = (norm_b * (1.0 + scale_b) + shift_b).astype(jnp.bfloat16).reshape(row_count, model_width)
    hidden_pre = matmul(modul_b, w_fc1) + b_fc1.astype(jnp.float32)
    hidden = gelu_tanh(hidden_pre).astype(jnp.bfloat16)
    branch_b = (matmul(hidden, w_fc2) + b_fc2.astype(jnp.float32)).reshape(latent_count, token_count, model_width)
    output = (middle + gate_b * branch_b).astype(jnp.bfloat16)
    back_mod, back_qkv, back_out, back_fc1, back_fc2 = fetch_back()
    grad_out = cot.astype(jnp.float32)
    grad_gate_b = lax.optimization_barrier(jnp.sum(grad_out * branch_b, 1))
    grad_branch_b = (grad_out * gate_b).reshape(row_count, model_width)
    branch_b_low = grad_branch_b.astype(jnp.bfloat16)
    grad_w_fc2 = matmul_tn(hidden, branch_b_low)
    grad_b_fc2 = lax.optimization_barrier(jnp.sum(grad_branch_b, 0))
    grad_hidden = matmul_nt(branch_b_low, back_fc2)
    gelu_value, gelu_back = jax.vjp(gelu_tanh, hidden_pre)
    grad_pre = gelu_back(grad_hidden)[0]
    grad_pre_low = grad_pre.astype(jnp.bfloat16)
    grad_w_fc1 = matmul_tn(modul_b, grad_pre_low)
    grad_b_fc1 = lax.optimization_barrier(jnp.sum(grad_pre, 0))
    grad_modul_b = matmul_nt(grad_pre_low, back_fc1).reshape(latent_count, token_count, model_width)
    grad_shift_b = lax.optimization_barrier(jnp.sum(grad_modul_b, 1))
    grad_scale_b = lax.optimization_barrier(jnp.sum(grad_modul_b * norm_b, 1))
    grad_middle = grad_out + norm_back(grad_modul_b * (1.0 + scale_b), norm_b, rstd_b)
    grad_gate_a = lax.optimization_barrier(jnp.sum(grad_middle * branch_a, 1))
    grad_branch_a = (grad_middle * gate_a).reshape(row_count, model_width)
    branch_a_low = grad_branch_a.astype(jnp.bfloat16)
    grad_w_out = matmul_tn(attn_flat, branch_a_low)
    grad_b_out = lax.optimization_barrier(jnp.sum(grad_branch_a, 0))
    grad_attended = matmul_nt(branch_a_low, back_out).astype(jnp.bfloat16).reshape(head_shape)
    again_scores = batched('lqhd,lkhd->lhqk', queries, keys_b) * 0.125
    again_probs = jnp.exp(again_scores - log_total)
    grad_values = batched('lhqk,lqhd->lkhd', again_probs.astype(jnp.bfloat16), grad_attended)
    grad_probs = batched('lqhd,lkhd->lhqk', grad_attended, values_b)
    delta_rows = batched('lqhd,lqhd->lhq', grad_attended, attended)
    grad_scores = (again_probs * (grad_probs - delta_rows[..., None]) * 0.125).astype(jnp.bfloat16)
    grad_queries = batched('lhqk,lkhd->lqhd', grad_scores, keys_b)
    grad_keys = batched('lhqk,lqhd->lkhd', grad_scores, queries)
    grad_proj = jnp.concatenate([grad_queries.reshape(row_count, model_width), grad_keys.reshape(row_count, model_width), grad_values.reshape(row_count, model_width)], 1)
    grad_proj_low = grad_proj.astype(jnp.bfloat16)
    grad_w_qkv = matmul_tn(modul_a, grad_proj_low)
    grad_b_qv = jnp.concatenate([lax.optimization_barrier(jnp.sum(grad_proj[:, :model_width], 0)), lax.optimization_barrier(jnp.sum(grad_proj[:, 2 * model_width:], 0))])
    grad_modul_a = matmul_nt(grad_proj_low, back_qkv).reshape(latent_count, token_count, model_width)
    grad_shift_a = lax.optimization_barrier(jnp.sum(grad_modul_a, 1))
    grad_scale_a = lax.optimization_barrier(jnp.sum(grad_modul_a * norm_a, 1))
    grad_inputs = grad_middle + norm_back(grad_modul_a * (1.0 + scale_a), norm_a, rstd_a)
    grad_modulation = jnp.concatenate([grad_shift_a, grad_scale_a, grad_gate_a, grad_shift_b, grad_scale_b, grad_gate_b], 1)
    grad_mod_low = grad_modulation.astype(jnp.bfloat16)
    grad_w_mod = matmul_tn(cond_act, grad_mod_low)
    grad_b_mod = lax.optimization_barrier(jnp.sum(grad_modulation, 0))
    grad_cond_act = matmul_nt(grad_mod_low, back_mod)
    silu_value, silu_back = jax.vjp(jax.nn.silu, cond_f)
    grad_cond = silu_back(grad_cond_act)[0]
    grads = (grad_w_mod, grad_b_mod, grad_w_qkv, grad_b_qv, grad_w_out, grad_b_out, grad_w_fc1, grad_b_fc1, grad_w_fc2, grad_b_fc2)
    return (output, grad_inputs, grad_cond, grads)

def reference(tokens, cond, cot, w_mod, b_mod, w_qkv, b_qv, w_out, b_out, w_fc1, b_fc1, w_fc2, b_fc2):
    weights = (w_mod, b_mod, w_qkv, b_qv, w_out, b_out, w_fc1, b_fc1, w_fc2, b_fc2)
    back_set = (w_mod, w_qkv, w_out, w_fc1, w_fc2)
    group_size = math.gcd(LATENTS, 16)
    group_count = LATENTS // group_size
    token_blocks = tokens.reshape(group_count, group_size, LAT_TOK, D)
    cond_blocks = cond.reshape(group_count, group_size, D)
    cot_blocks = cot.reshape(group_count, group_size, LAT_TOK, D)

    def scan_step(running, inputs_blk):
        token_blk, cond_blk, cot_blk = inputs_blk
        output, grad_inputs, grad_cond, grads = block_pass(token_blk, cond_blk, cot_blk, weights, lambda: back_set)
        running = tuple((total_val + grad_val for total_val, grad_val in zip(running, grads)))
        return (running, (output, grad_inputs, grad_cond))
    start = tuple((jnp.zeros(weight.shape, jnp.float32) for weight in weights))
    totals, stacked = lax.scan(scan_step, start, (token_blocks, cond_blocks, cot_blocks))
    mixed = stacked[0].reshape(TOKENS, D)
    grad_tokens = stacked[1].reshape(TOKENS, D)
    grad_cond = stacked[2].reshape(LATENTS, D)
    return (mixed, grad_tokens, grad_cond, totals[0], totals[1], totals[2], totals[3], totals[4], totals[5], totals[6], totals[7], totals[8], totals[9])
```

```python
import functools

import jax
import jax.numpy as jnp
from jax import lax
from jax.experimental import pallas as pl
from jax.experimental.pallas import tpu as pltpu
from jax.sharding import PartitionSpec as P


BF = jnp.bfloat16
F32 = jnp.float32
ANY = pl.BlockSpec(memory_space=pl.ANY)
VM = pl.BlockSpec(memory_space=pltpu.VMEM)
SM = pl.BlockSpec(memory_space=pltpu.SMEM)
CHUNK = 512


def dot(left, right):
    return jnp.dot(left, right, preferred_element_type=F32)


def dot_tn(left, right):
    return lax.dot_general(left, right, (((0,), (0,)), ((), ())), preferred_element_type=F32)


def dot_nt(left, right):
    return lax.dot_general(left, right, (((1,), (1,)), ((), ())), preferred_element_type=F32)


def layer_norm(values):
    center = values - jnp.mean(values, -1, keepdims=True)
    rstd_val = lax.rsqrt(jnp.mean(center * center, -1, keepdims=True) + 1e-06)
    return (center * rstd_val, rstd_val)


def norm_back(grad_norm, normed, rstd_val):
    return rstd_val * (
        grad_norm
        - jnp.mean(grad_norm, -1, keepdims=True)
        - normed * jnp.mean(grad_norm * normed, -1, keepdims=True)
    )


def column_sum(values):
    return jnp.sum(values, 0, keepdims=True)


class Place:
    def __init__(self, mesh):
        self.ns = mesh.shape["shard"]
        self.nr = mesh.shape["replica"]
        self.s = lax.axis_index("shard")
        self.r = lax.axis_index("replica")
        self.c = lax.rem(self.r, 2)
        self.z1 = lax.rem(self.r // 2, 2)
        self.sbits = self.ns.bit_length() - 1
        self.rbits = self.nr.bit_length() - 1
        self.index = jnp.stack([self.s, self.c, self.z1]).astype(jnp.int32)

    def shard(self, value, k):
        return lax.ppermute(value, "shard", [(i, i ^ k) for i in range(self.ns)])

    def replica(self, value, k):
        return lax.ppermute(value, "replica", [(i, i ^ k) for i in range(self.nr)])


def after(value, *gates):
    return lax.optimization_barrier((value, *gates))[0]


def cost(flops, nbytes):
    return pl.CostEstimate(flops=int(flops), bytes_accessed=int(nbytes), transcendentals=0)


def size_of(arrays):
    return sum(a.size * a.dtype.itemsize for a in arrays)


def call(name, kernel, outs, ins, specs, scratch, flops, vmem=58 << 20):
    return pl.pallas_call(
        kernel,
        out_shape=[jax.ShapeDtypeStruct(*o) for o in outs],
        in_specs=specs,
        out_specs=[VM] * len(outs),
        scratch_shapes=scratch,
        cost_estimate=cost(flops, size_of(ins) + sum(jnp.zeros((), o[1]).dtype.itemsize * o[0][0] * o[0][-1] for o in outs)),
        compiler_params=pltpu.CompilerParams(vmem_limit_bytes=vmem),
        name=name,
    )(*ins)


class Gather:
    def __init__(self, place, owns, bits):
        self.place, self.owns, self.bits = place, owns, bits
        self.size = owns[0].shape[0] // 2

    def first(self, *gates):
        place = self.place
        parts = [lax.dynamic_slice_in_dim(w, place.c * self.size, self.size, 0) for w in self.owns]
        own = parts[0] if len(parts) == 1 else jnp.concatenate(parts, 1)
        if gates:
            own = after(own, *gates)
        self.own = own
        self.got = {1 << self.bits[0]: place.shard(own, 1 << self.bits[0])}
        if len(self.bits) > 1:
            self.got[1 << self.bits[1]] = place.shard(own, 1 << self.bits[1])
        return self.got[1 << self.bits[0]]

    def second(self):
        place = self.place
        seen = [1 << self.bits[0]] if self.bits else []
        for at, b in enumerate(self.bits[1:]):
            k = 1 << b
            if k not in self.got:
                self.got[k] = place.shard(self.own, k)
            for key in list(seen):
                self.got[key ^ k] = place.shard(self.got[key], k)
            seen = seen + [k] + [key ^ k for key in seen]

    def third(self):
        self.keys = sorted(self.got)
        self.near = [self.got[k] for k in self.keys]
        self.far = [self.place.replica(v, 1) for v in self.near]
        return list(self.owns) + self.near + self.far

    def width(self):
        return sum(w.shape[1] for w in self.owns)

    def shape(self):
        return (self.owns[0].shape[0] * self.place.ns, self.width())


class Loader:
    def __init__(self, gather):
        self.rows, self.size = gather.owns[0].shape[0], gather.size
        self.widths = [w.shape[1] for w in gather.owns]
        self.keys = gather.keys
        self.count = len(gather.owns) + 2 * len(gather.keys)
        self.scratch = [pltpu.VMEM(gather.shape(), BF), pltpu.SemaphoreType.DMA((self.count,))]

    def copies(self, idx, pieces, full, sem, lo=0, hi=None):
        hi = sum(self.widths) if hi is None else hi
        s, c = idx[0], idx[1]
        out, at = [], 0
        n = len(self.widths)
        for i, w in enumerate(self.widths):
            if lo <= at and at + w <= hi:
                row = pl.multiple_of(s * self.rows, 16)
                out.append((pieces[i], full.at[pl.ds(row, self.rows), pl.ds(at - lo, w)], i))
            at += w
        for side in range(2):
            for j, k in enumerate(self.keys):
                i = n + side * len(self.keys) + j
                half = c if side == 0 else 1 - c
                row = pl.multiple_of(jnp.bitwise_xor(s, k) * self.rows + half * self.size, 16)
                out.append((pieces[i].at[:, pl.ds(lo, hi - lo)], full.at[pl.ds(row, self.size), :], i))
        return [pltpu.make_async_copy(a, b, sem.at[i]) for a, b, i in out]


def attention_kernel(loader, width, *refs):
    idx, tokens, mod, bqv, bo = refs[:5]
    pieces = refs[5 : 5 + loader.count]
    packed, qkv, lse, branch, full, sem = refs[5 + loader.count :]
    copies = loader.copies(idx, pieces, full, sem)
    for copy in copies:
        copy.start()
    inputs = tokens[...].astype(F32)
    part = lambda i: mod[:, i * width : (i + 1) * width]
    norm_a, _ = layer_norm(inputs)
    modul_a = (norm_a * (1.0 + part(1)) + part(0)).astype(BF)
    packed[:, :width] = modul_a
    for copy in copies:
        copy.wait()
    qkv[:, :width] = (dot(modul_a, full[:, :width]) + bqv[:, :width]).astype(BF)
    qkv[:, width : 2 * width] = dot(modul_a, full[:, width : 2 * width]).astype(BF)
    qkv[:, 2 * width : 3 * width] = (
        dot(modul_a, full[:, 2 * width : 3 * width]) + bqv[:, width:]
    ).astype(BF)

    def pair(p, carry):
        at = pl.multiple_of(p * 128, 128)
        q = qkv[:, pl.ds(at, 128)]
        k = qkv[:, pl.ds(width + at, 128)]
        v = qkv[:, pl.ds(2 * width + at, 128)]
        outs = []
        for h in range(2):
            lanes = slice(64 * h, 64 * h + 64)
            scores = dot_nt(q[:, lanes], k[:, lanes]) * 0.125
            row_max = jnp.max(scores, -1, keepdims=True)
            exp_scores = jnp.exp(scores - row_max)
            row_total = jnp.sum(exp_scores, -1, keepdims=True)
            log_total = row_max + jnp.log(row_total)
            lse[:, pl.ds(pl.multiple_of(2 * at + 128 * h, 128), 128)] = jnp.broadcast_to(
                log_total, (q.shape[0], 128)
            )
            probs = (exp_scores * (1.0 / row_total)).astype(BF)
            outs.append(dot(probs, v[:, lanes]))
        packed[:, pl.ds(width + at, 128)] = jnp.concatenate(outs, 1).astype(BF)
        return carry

    lax.fori_loop(0, width // 128, pair, 0)
    branch_a = dot(packed[:, width : 2 * width], full[:, 3 * width :]) + bo[...]
    branch[...] = branch_a
    middle = inputs + part(2) * branch_a
    norm_b, _ = layer_norm(middle)
    packed[:, 2 * width :] = (norm_b * (1.0 + part(4)) + part(3)).astype(BF)


def hidden_kernel(loader, width, *refs):
    idx, packed, cot, mod, b1 = refs[:5]
    pieces = refs[5 : 5 + loader.count]
    out, slope, own_right, full, sem = refs[5 + loader.count :]
    copies = loader.copies(idx, pieces, full, sem)
    for copy in copies:
        copy.start()
    hidden_width = full.shape[1]
    half = width // 2
    low = (cot[...].astype(F32) * mod[:, 5 * width :]).astype(BF)
    first = idx[1] == 0
    own_right[...] = jnp.where(first, low[:, :half], low[:, half:])
    out[:, hidden_width:] = jnp.where(first, low[:, half:], low[:, :half])
    modul_b = packed[:, 2 * width :]
    for copy in copies:
        copy.wait()

    def chunk(j, carry):
        at = pl.ds(pl.multiple_of(j * CHUNK, 128), CHUNK)
        u = dot(modul_b, full[:, at]) + b1[:, at]
        scale = 0.7978845608028654
        tanh = jnp.tanh(scale * (u + 0.044715 * (u * u * u)))
        out[:, at] = (0.5 * u * (1.0 + tanh)).astype(BF)
        slope[:, at] = 0.5 * (1.0 + tanh) + 0.5 * u * (1.0 - tanh * tanh) * (
            scale * (1.0 + 3.0 * 0.044715 * (u * u))
        )
        return carry

    lax.fori_loop(0, hidden_width // CHUNK, chunk, 0)


def pre_kernel(loader, width, *refs):
    idx, cot, mod, slope = refs[:4]
    pieces = refs[4 : 4 + loader.count]
    lows, sums, full, sem = refs[4 + loader.count :]
    copies = loader.copies(idx, pieces, full, sem)
    for copy in copies:
        copy.start()
    hidden_width = full.shape[0]
    per_half = hidden_width // 2 // CHUNK
    low = (cot[...].astype(F32) * mod[:, 5 * width :]).astype(BF)
    for copy in copies:
        copy.wait()

    def chunk(j, carry):
        at = pl.multiple_of(j * CHUNK, 128)
        grad = dot_nt(low, full[pl.ds(at, CHUNK), :]) * slope[:, pl.ds(at, CHUNK)]
        sums[:, pl.ds(at, CHUNK)] = column_sum(grad)
        which = jnp.bitwise_xor(j // per_half, idx[1])
        within = pl.multiple_of(lax.rem(j, per_half) * CHUNK, 128)
        lows[which, :, pl.ds(within, CHUNK)] = grad.astype(BF)
        return carry

    lax.fori_loop(0, hidden_width // CHUNK, chunk, 0)


def mixed_kernel(loader, width, *refs):
    idx, hidden, tokens, cot, mod, branch, b2 = refs[:7]
    pieces = refs[7 : 7 + loader.count]
    mixed, gate_sum, bias_sum, full, sem = refs[7 + loader.count :]
    copies = loader.copies(idx, pieces, full, sem)
    for copy in copies:
        copy.start()
    for copy in copies:
        copy.wait()
    gate_b = mod[:, 5 * width :]
    branch_b = dot(hidden[:, : full.shape[0]], full[...]) + b2[...]
    middle = tokens[...].astype(F32) + mod[:, 2 * width : 3 * width] * branch[...]
    mixed[...] = (middle + gate_b * branch_b).astype(BF)
    grad_out = cot[...].astype(F32)
    gate_sum[...] = column_sum(grad_out * branch_b)
    bias_sum[...] = column_sum(grad_out * gate_b)


def back_kernel(fc1, first, width, *refs):
    idx, tokens, cot, mod, branch, lows, packed, qkv, lse = refs[:9]
    pieces1 = refs[9 : 9 + fc1.count]
    pieces_a = refs[9 + fc1.count : 9 + fc1.count + first.count]
    rest = refs[9 + fc1.count + first.count :]
    proj_out, rights, middle_out, vec, vec_qv, full1, sem1, full_o, sem_o, attn_grad = rest
    copies = fc1.copies(idx, pieces1, full1, sem1)
    copies_o = first.copies(idx, pieces_a, full_o, sem_o, 3 * width, 4 * width)
    for copy in copies + copies_o:
        copy.start()
    c = idx[1]
    part = lambda i: mod[:, i * width : (i + 1) * width]
    grad_out = cot[...].astype(F32)
    branch_a = branch[...]
    middle = tokens[...].astype(F32) + part(2) * branch_a
    norm_b, rstd_b = layer_norm(middle)
    for copy in copies:
        copy.wait()
    half = full1.shape[1] // 2
    lo = jnp.where(c == 0, 0, 1)
    grad_modul_b = dot_nt(lows[lo], full1[:, :half]) + dot_nt(lows[1 - lo], full1[:, half:])
    vec[0:1, :] = column_sum(grad_modul_b)
    vec[1:2, :] = column_sum(grad_modul_b * norm_b)
    grad_middle = grad_out + norm_back(grad_modul_b * (1.0 + part(4)), norm_b, rstd_b)
    middle_out[...] = grad_middle
    vec[2:3, :] = column_sum(grad_middle * branch_a)
    grad_branch_a = grad_middle * part(2)
    vec[3:4, :] = column_sum(grad_branch_a)
    vec[4:, :] = jnp.zeros((4, width), F32)
    low = grad_branch_a.astype(BF)
    for copy in copies_o:
        copy.wait()
    attn_grad[...] = dot_nt(low, full_o[...]).astype(BF)

    def pair(p, carry):
        at = pl.multiple_of(p * 128, 128)
        q = qkv[:, pl.ds(at, 128)]
        k = qkv[:, pl.ds(width + at, 128)]
        v = qkv[:, pl.ds(2 * width + at, 128)]
        grad = attn_grad[:, pl.ds(at, 128)]
        product = grad.astype(F32) * packed[:, pl.ds(width + at, 128)].astype(F32)
        outs = []
        for h in range(2):
            lanes = slice(64 * h, 64 * h + 64)
            qh, kh, vh, gh = q[:, lanes], k[:, lanes], v[:, lanes], grad[:, lanes]
            total = lse[:, pl.ds(pl.multiple_of(2 * at + 128 * h, 128), 128)][:, :1]
            probs = jnp.exp(dot_nt(qh, kh) * 0.125 - total)
            delta = jnp.sum(product[:, lanes], -1, keepdims=True)
            grad_scores = (probs * (dot_nt(gh, vh) - delta) * 0.125).astype(BF)
            outs.append((dot(grad_scores, kh), dot_tn(grad_scores, qh), dot_tn(probs.astype(BF), gh)))
        both = [jnp.concatenate([outs[0][i], outs[1][i]], 1) for i in range(3)]
        for i in range(3):
            proj_out[:, pl.ds(i * width + at, 128)] = both[i].astype(BF)
        vec_qv[:, pl.ds(at, 128)] = column_sum(both[0])
        vec_qv[:, pl.ds(width + at, 128)] = column_sum(both[2])
        return carry

    lax.fori_loop(0, width // 128, pair, 0)
    wide, narrow = 3 * width // 2, width // 2
    for which in range(2):
        at = pl.multiple_of(jnp.bitwise_xor(c, which) * wide, 128)
        rights[which, :, :wide] = proj_out[:, pl.ds(at, wide)]
    is_first = c == 0
    rights[0, :, wide:] = jnp.where(is_first, low[:, :narrow], low[:, narrow:])
    rights[1, :, wide:] = jnp.where(is_first, low[:, narrow:], low[:, :narrow])


def tokens_kernel(loader, width, *refs):
    idx, tokens, mod, proj, grad_middle = refs[:5]
    pieces = refs[5 : 5 + loader.count]
    out, vec, full, sem = refs[5 + loader.count :]
    copies = loader.copies(idx, pieces, full, sem, 0, 3 * width)
    for copy in copies:
        copy.start()
    norm_a, rstd_a = layer_norm(tokens[...].astype(F32))
    for copy in copies:
        copy.wait()
    grad_modul_a = dot_nt(proj[...], full[...])
    vec[0:1, :] = column_sum(grad_modul_a)
    vec[1:2, :] = column_sum(grad_modul_a * norm_a)
    vec[2:, :] = jnp.zeros((6, width), F32)
    scale_a = mod[:, width : 2 * width]
    out[...] = grad_middle[...] + norm_back(grad_modul_a * (1.0 + scale_a), norm_a, rstd_a)


def split_kernel(plan, parts, ns, counts, *refs):
    idx = refs[0]
    n_left, n_right = counts
    lefts = refs[1 : 1 + n_left]
    rights = refs[1 + n_left : 1 + n_left + n_right]
    outs, total = refs[1 + n_left + n_right : -1], refs[-1]
    depth = total.shape[0]
    block = depth // ns
    for source, left_at, right_at, cols in parts:
        x0 = lefts[source[0]][:, left_at : left_at + depth]
        x1 = lefts[source[1]][:, left_at : left_at + depth]
        step = 384
        for at in range(right_at, right_at + cols, step):
            y0 = rights[0][0, :, at : at + step] if rights[0].ndim == 3 else rights[0][:, at : at + step]
            y1 = rights[1][:, at : at + step]
            total[:, at : at + step] = (dot_tn(x0, y0) + dot_tn(x1, y1)).astype(BF)
    for i, (row, rows, bit) in enumerate(plan):
        send, keep = outs[2 * i], outs[2 * i + 1]
        places = [0, 0]
        for k in range(ns):
            side = (k >> bit) & 1
            at = pl.multiple_of(jnp.bitwise_xor(idx[0], k) * block + row, 16)
            (keep, send)[side][places[side]] = total[pl.ds(at, rows), :]
            places[side] += 1


def split_tall_kernel(bit, ns, idx, left0, left1, right0, right1, send, keep, total):
    depth = total.shape[0]
    block = depth // ns
    tile = 256

    def chunk(j, carry):
        at = pl.ds(pl.multiple_of(j * tile, 128), tile)
        value = dot_tn(left0[:, at], right0[...]) + dot_tn(left1[:, at], right1[...])
        total[at, :] = value.astype(BF)
        return carry

    lax.fori_loop(0, depth // tile, chunk, 0)
    places = [0, 0]
    for k in range(ns):
        side = (k >> bit) & 1
        at = pl.multiple_of(jnp.bitwise_xor(idx[0], k) * block, 16)
        (keep, send)[side][places[side]] = total[pl.ds(at, block), :]
        places[side] += 1


def add(*values):
    total = values[0].astype(F32)
    for value in values[1:]:
        total = total + value.astype(F32)
    return total


def reduce_shards(place, send, keep, bits):
    labels = [k for k in range(place.ns) if not (k >> bits[0]) & 1]
    got = place.shard(send, 1 << bits[0])
    terms = [keep, got]
    for b in bits[1:]:
        away = [i for i, k in enumerate(labels) if (k >> b) & 1]
        stay = [i for i, k in enumerate(labels) if not (k >> b) & 1]
        take = lambda t, ids: jnp.stack([t[i] for i in ids], 0) if len(ids) > 1 else t[ids[0]][None]
        moved = add(*[take(t, away) for t in terms]).astype(BF)
        terms = [take(t, stay) for t in terms] + [place.shard(moved, 1 << b)]
        labels = [labels[i] for i in stay]
    return [t[0] for t in terms]


def reduce_replicas(place, keep, send):
    cur = add(keep, place.replica(send, 2)).astype(BF)
    for b in range(2, place.rbits):
        cur = add(cur, place.replica(cur, 1 << b)).astype(BF)
    near = place.replica(cur, 2)
    return [cur, near, place.replica(cur, 1), place.replica(near, 1)]


def halves(place, terms):
    rows = terms[0].shape[0] // 2
    pick = lambda z: add(*[lax.dynamic_slice_in_dim(t, z * rows, rows, 0) for t in terms]).astype(BF)
    return pick(place.z1), pick(1 - place.z1)


def place_kernel(cuts, idx, q0, q1, q2, q3, *outs):
    rows = q0.shape[0]
    c, z = idx[1], idx[2]
    for flip_z, flip_c, ref in ((0, 0, q0), (1, 0, q1), (0, 1, q2), (1, 1, q3)):
        row = pl.multiple_of(jnp.bitwise_xor(z, flip_z) * rows, 16)
        at = 0
        for cols, out in zip(cuts, outs):
            col = pl.multiple_of(jnp.bitwise_xor(c, flip_c) * cols, 128)
            out[pl.ds(row, rows), pl.ds(col, cols)] = ref[:, at : at + cols].astype(F32)
            at += cols


def place_gradient(place, quads, cuts):
    rows = 2 * quads[0].shape[0]
    outs = [((rows, 2 * cols), F32) for cols in cuts]
    return call("place", functools.partial(place_kernel, cuts), outs, [place.index] + quads, [SM] + [VM] * 4, [], 0)


def body(mesh, tokens, cond, cot, w_mod, b_mod, w_qkv, b_qv, w_out, b_out, w_fc1, b_fc1, w_fc2, b_fc2):
    place = Place(mesh)
    ns, idx = place.ns, place.index
    rows, width = tokens.shape
    hidden_width = w_fc1.shape[1]
    up, down = list(range(place.sbits)), list(range(place.sbits))[::-1]

    cond_f = cond.astype(F32)
    cond_act = jax.nn.silu(cond_f).astype(BF)
    biases = (b_mod, b_qv, b_out, b_fc1, b_fc2)
    small = jnp.concatenate([v.astype(F32).reshape(1, -1) for v in (cond_act,) + biases], 1)
    held = small
    for b in up:
        held = jnp.concatenate([held, place.shard(held, 1 << b)], 0)
    g_a = Gather(place, [w_qkv, w_out], up)
    g_1 = Gather(place, [w_fc1], down)
    g_2 = Gather(place, [w_fc2], up)
    got_a = g_a.first()
    g_a.second()
    got_1 = g_1.first(got_a)
    g_1.second()
    g_2.first(got_1)
    g_2.second()

    conds = held[:, :width].astype(BF)
    my_rows = w_mod.shape[0]
    part = dot(lax.dynamic_slice_in_dim(conds, place.s * my_rows, my_rows, 1), w_mod)
    for b in down:
        n = part.shape[0] // 2
        part = part[:n] + place.shard(part[n:], 1 << b)
    ordered = held[:, width:]
    for b in up:
        flipped = jnp.stack([ordered[k ^ (1 << b)] for k in range(ns)], 0)
        ordered = jnp.where(lax.rem(place.s // (1 << b), 2) == 1, flipped, ordered)
    full_bias, at = [], 0
    for v in biases:
        n = v.shape[0]
        full_bias.append(ordered[:, at : at + n].reshape(1, ns * n))
        at += n
    bm, bqv, bo, b1, b2 = full_bias
    mod = part + bm

    pieces_a = g_a.third()
    load_a = Loader(g_a)
    packed, qkv, lse, branch = call("attend",
        functools.partial(attention_kernel, load_a, width),
        [((rows, 3 * width), BF), ((rows, 3 * width), BF), ((rows, 2 * width), F32), ((rows, width), F32)],
        [idx, tokens, mod, bqv, bo] + pieces_a,
        [SM] + [VM] * 4 + [ANY] * load_a.count,
        load_a.scratch,
        2 * rows * width * 4 * width + 4 * rows * rows * width,
    )
    packed_other = place.replica(packed, 1)
    pieces_1 = g_1.third()
    load_1 = Loader(g_1)
    half = width // 2
    hidden, slope, right_2 = call("hidden",
        functools.partial(hidden_kernel, load_1, width),
        [((rows, hidden_width + half), BF), ((rows, hidden_width), F32), ((rows, half), BF)],
        [idx, packed, cot, mod, b1] + pieces_1,
        [SM] + [VM] * 4 + [ANY] * load_1.count,
        load_1.scratch,
        2 * rows * width * hidden_width,
    )
    hidden_other = place.replica(hidden, 1)

    block = hidden_width // ns

    def tall(idx_ref, l0, l1, r0, send, keep, total):
        split_tall_kernel(0, ns, idx_ref, l0, l1, r0, l1.at[:, pl.ds(hidden_width, half)], send, keep, total)

    send, keep = call("grad_fc2",
        tall,
        [((ns // 2, block, half), BF), ((ns // 2, block, half), BF)],
        [idx, hidden, hidden_other, right_2],
        [SM] + [VM] * 3,
        [pltpu.VMEM((hidden_width, half), BF)],
        4 * rows * half * hidden_width,
    )
    quads_2 = reduce_replicas(place, *halves(place, reduce_shards(place, send, keep, up)))
    (grad_w_fc2,) = place_gradient(place, quads_2, (half,))

    pieces_2 = g_2.third()
    load_2 = Loader(g_2)
    lows, sums_1 = call("grad_pre",
        functools.partial(pre_kernel, load_2, width),
        [((2, rows, hidden_width // 2), BF), ((1, hidden_width), F32)],
        [idx, cot, mod, slope] + pieces_2,
        [SM] + [VM] * 3 + [ANY] * load_2.count,
        load_2.scratch,
        2 * rows * width * hidden_width,
    )
    lows_other = place.replica(lows[1], 1)
    wide = hidden_width // 2
    block = width // ns
    send, keep = call("grad_fc1",
        functools.partial(
            split_kernel, ((0, block, down[0]),), (((0, 1), 2 * width, 0, wide),), ns, (2, 2)
        ),
        [((ns // 2, block, wide), BF), ((ns // 2, block, wide), BF)],
        [idx, packed, packed_other, lows, lows_other],
        [SM] + [VM] * 4,
        [pltpu.VMEM((width, wide), BF)],
        4 * rows * width * wide,
    )
    quads_1 = reduce_replicas(place, *halves(place, reduce_shards(place, send, keep, down)))
    (grad_w_fc1,) = place_gradient(place, quads_1, (wide,))

    proj, rights, grad_middle, vec, vec_qv = call("back",
        functools.partial(back_kernel, load_1, load_a, width),
        [
            ((rows, 3 * width), BF),
            ((2, rows, 2 * width), BF),
            ((rows, width), F32),
            ((8, width), F32),
            ((1, 2 * width), F32),
        ],
        [idx, tokens, cot, mod, branch, lows, packed, qkv, lse] + pieces_1 + pieces_a,
        [SM] + [VM] * 8 + [ANY] * (load_1.count + load_a.count),
        load_1.scratch
        + [pltpu.VMEM((width, width), BF), load_a.scratch[1], pltpu.VMEM((rows, width), BF)],
        2 * rows * width * (hidden_width + width) + 10 * rows * rows * width,
    )
    rights_other = place.replica(rights[1], 1)
    wide_a = 2 * width
    side = block // 2
    plan = ((0, side, up[0]), (side, side, down[0]))
    cut = 3 * width // 2
    outs = call("grad_qkv_out",
        functools.partial(
            split_kernel,
            plan,
            (((0, 1), 0, 0, cut), ((0, 1), width, cut, wide_a - cut)),
            ns,
            (2, 2),
        ),
        [((ns // 2, side, wide_a), BF)] * 4,
        [idx, packed, packed_other, rights, rights_other],
        [SM] + [VM] * 4,
        [pltpu.VMEM((width, wide_a), BF)],
        4 * rows * width * wide_a,
    )
    top = reduce_shards(place, outs[0], outs[1], up)
    low = reduce_shards(place, outs[2], outs[3], down)
    top, low = add(*top).astype(BF), add(*low).astype(BF)
    keep = jnp.where(place.z1 == 0, top, low)
    send = jnp.where(place.z1 == 0, low, top)
    quads_a = reduce_replicas(place, keep, send)
    grad_w_qkv, grad_w_out = place_gradient(place, quads_a, (cut, wide_a - cut))

    grad_tokens, vec_a = call("tokens",
        functools.partial(tokens_kernel, load_a, width),
        [((rows, width), F32), ((8, width), F32)],
        [idx, tokens, mod, proj, grad_middle] + pieces_a,
        [SM] + [VM] * 4 + [ANY] * load_a.count,
        [pltpu.VMEM((width, 3 * width), BF), load_a.scratch[1]],
        6 * rows * width * width,
    )
    mixed, gate_sum, sums_2 = call("mixed",
        functools.partial(mixed_kernel, load_2, width),
        [((rows, width), BF), ((1, width), F32), ((1, width), F32)],
        [idx, hidden, tokens, cot, mod, branch, b2] + pieces_2,
        [SM] + [VM] * 6 + [ANY] * load_2.count,
        load_2.scratch,
        2 * rows * width * hidden_width,
    )

    grad_mod = jnp.concatenate([vec_a[0:1], vec_a[1:2], vec[2:3], vec[0:1], vec[1:2], gate_sum], 1)
    held = jnp.concatenate([grad_mod.astype(BF).astype(F32), cond_act.astype(F32)], 1)
    vectors = (grad_mod, vec_qv, vec[3:4], sums_1, sums_2)
    terms = jnp.concatenate([v.reshape(ns, v.shape[1] // ns) for v in vectors], 1)
    for b in up:
        flipped = jnp.stack([terms[k ^ (1 << b)] for k in range(ns)], 0)
        terms = jnp.where(lax.rem(place.s // (1 << b), 2) == 1, flipped, terms)
    wide_m = held.shape[1]

    def exchange(permute, held, kept, sent):
        n, m = held.shape[0], sent.shape[0]
        both = permute(jnp.concatenate([held.reshape(1, -1), sent.reshape(1, -1)], 1))
        return both[:, : n * wide_m].reshape(n, wide_m), kept + both[:, n * wide_m :].reshape(m, -1)

    for b in down:
        n = terms.shape[0] // 2
        other, terms = exchange(lambda v: place.shard(v, 1 << b), held, terms[:n], terms[n:])
        held = jnp.concatenate([held, other], 0)
    group = held
    for b in reversed(range(place.rbits)):
        other, terms = exchange(lambda v: place.replica(v, 1 << b), held, terms, terms)
        bit = lax.rem(place.r // (1 << b), 2)
        held = jnp.where(bit == 0, jnp.concatenate([held, other], 0), jnp.concatenate([other, held], 0))
    held = held.astype(BF)
    my_conds = lax.dynamic_slice_in_dim(
        held[:, 6 * width :], place.s * my_rows, my_rows, 1
    )
    grad_w_mod = dot_tn(my_conds, held[:, : 6 * width])
    bias_grads, at = [], 0
    for v in biases:
        bias_grads.append(terms[0, at : at + v.shape[0]])
        at += v.shape[0]

    part = dot_nt(group[:, : 6 * width].astype(BF), w_mod)
    labels = [0]
    for b in down:
        labels = labels + [k ^ (1 << b) for k in labels]
    mine = [None] * ns
    for i, k in enumerate(labels):
        mine[k] = part[i] if k == 0 else place.shard(part[i], k)
    mine = jnp.stack(mine, 0)
    for b in up:
        flipped = jnp.stack([mine[k ^ (1 << b)] for k in range(ns)], 0)
        mine = jnp.where(lax.rem(place.s // (1 << b), 2) == 1, flipped, mine)
    silu_value, silu_back = jax.vjp(jax.nn.silu, cond_f)
    grad_cond = silu_back(mine.reshape(1, width))[0]
    g_bmod, g_bqv, g_bout, g_bfc1, g_bfc2 = bias_grads
    return (
        mixed,
        grad_tokens,
        grad_cond,
        grad_w_mod,
        g_bmod,
        grad_w_qkv,
        g_bqv,
        grad_w_out,
        g_bout,
        grad_w_fc1,
        g_bfc1,
        grad_w_fc2,
        g_bfc2,
    )


def solution(mesh):
    both = P(("shard", "replica"), None)
    matrix, vector = P("shard", None), P("shard")
    return jax.shard_map(
        functools.partial(body, mesh),
        mesh=mesh,
        in_specs=(both, both, both) + (matrix, vector) * 5,
        out_specs=(both, both, both) + (matrix, vector) * 5,
        check_vma=False,
    )
```
